256 devices in a mesh: dp: 16 (over x, y), expert: 16 (over z, core).
Axes of the slice: x: 4, y: 4, z: 8, core: 2. Of those that a mesh axis runs over, the one named last changes fastest.
Arguments:
- tokens: bfloat16 [49152, 2048], P(('dp', 'expert')), may hold values from -6 to 6
- modality: int32 [49152], P(('dp', 'expert')), may hold values from 0 to 1, as said below
- local_expert: int32 [49152], P(('dp', 'expert')), may hold values from 0 to 1, as said below
- combine_weight: float32 [49152], P(('dp', 'expert')), may hold values from 0.3 to 1
- norm_gain: float32 [2, 2048], replicated, may hold values from 0.1 to 1.9
- gate_weight: bfloat16 [2048, 16384], P('dp', 'expert'), may hold values from -0.125 to 0.125
- up_weight: bfloat16 [2048, 16384], P('dp', 'expert'), may hold values from -0.125 to 0.125
- down_weight: bfloat16 [16384, 2048], P('expert', 'dp'), may hold values from -0.09375 to 0.09375
Outputs:
- mixed: bfloat16 [49152, 2048], P(('dp', 'expert'))
The draws below stay inside these ranges and needn't reach their ends.
Inputs may be any that keep to these rules, and one draw needn't show every extreme that they name: Expert e = modality * 2 + local_expert. Among the 192 rows of each device (aligned blocks in order) no expert is chosen by more than 72 rows, and on every device one expert is chosen by exactly 72. `local_expert`: drawn together with modality under the bound stated there.
All inputs are finite; a program needn't handle non-finite values.
Results may differ from the reference program's by a relative error of at most 0.005.
Values may be sent and summed in bfloat16 or wider, within the bound.
No kernel may reach another device: no remote copies, remote signals or barrier semaphores. Data moves between devices by JAX's collectives and lax.ppermute only.
A program may use at most 64 MiB of HBM per device.

```python
import jax
import jax.numpy as jnp
from jax import lax

D = 2048
H = 4096
EXP_MOD = 2
EXPERTS = 4
TOK_DEV = 192
CAP = 72
TOKENS = 49152
N_EXPERT = 16


def routing(key):
    blocks = TOKENS // TOK_DEV
    block_keys = jax.random.split(jax.random.fold_in(key, 7), blocks)

    def one_block(block_key):
        key_counts, key_order, key_rank = jax.random.split(block_key, 3)
        count_keys = jax.random.split(key_counts, EXPERTS)
        count_list = [jnp.int32(CAP)]
        remaining = jnp.int32(TOK_DEV - CAP)
        for step_index in range(EXPERTS - 2):
            slots_after = EXPERTS - 2 - step_index
            low_bound = jnp.maximum(1, remaining - slots_after * CAP)
            high_bound = jnp.minimum(CAP, remaining - slots_after)
            chosen = jax.random.randint(count_keys[step_index], (), low_bound, high_bound + 1, dtype=jnp.int32)
            count_list.append(chosen)
            remaining = remaining - chosen
        count_list.append(remaining)
        counts = jnp.stack(count_list).astype(jnp.int32)
        expert_order = jax.random.permutation(key_order, EXPERTS).astype(jnp.int32)
        bounds_cum = jnp.cumsum(counts)
        row_rank = jax.random.permutation(key_rank, TOK_DEV).astype(jnp.int32)
        slot_group = jnp.sum((row_rank[:, None] >= bounds_cum[None, :]).astype(jnp.int32), axis=1)
        return expert_order[slot_group]
    return jax.vmap(one_block)(block_keys).reshape(TOKENS).astype(jnp.int32)


def draw_modality(key, part):
    return (routing(key) // EXP_MOD).astype(jnp.int32)


def draw_local_expert(key, part):
    return (routing(key) % EXP_MOD).astype(jnp.int32)


def block_scale(own_key, shape, cuts, low, top_value):
    loudness = 1.0
    for axis_at, parts in cuts:
        draws = jax.random.uniform(jax.random.fold_in(jax.random.fold_in(own_key, 6), axis_at), (parts,), jnp.float32, low / len(cuts), top_value / len(cuts))
        loudness = loudness * jnp.repeat(jnp.exp(draws), shape[axis_at] // parts).reshape((-1,) + (1,) * (len(shape) - 1 - axis_at))
    return loudness


def gaussian(rng, shape, spread, reach, cuts=(), held_as=jnp.bfloat16):
    gain = block_scale(rng, shape, cuts, -0.22, 0.18) if cuts else 1.0
    drawn = jax.random.normal(rng, shape, jnp.float32) * spread * gain
    return jnp.minimum(jnp.maximum(drawn, -reach), reach).astype(held_as)


def setup_inputs(seed: int = 0) -> dict:
    streams_of = jax.random.split(jax.random.key(seed), 9)
    tokens = gaussian(streams_of[0], (TOKENS, D), 1.0, 6.0, ((0, 256),))
    modality = draw_modality(jax.random.fold_in(streams_of[8], 71), 0)
    local_expert = draw_local_expert(jax.random.fold_in(streams_of[8], 71), 0)
    combine_weight = jnp.clip(0.3 + 0.7 * jax.random.uniform(streams_of[3], (TOKENS,), jnp.float32) ** block_scale(streams_of[3], (TOKENS,), ((0, 256),), -0.2, 0.2), 0.3, 1.0)
    norm_gain = jnp.clip(1.0 + 0.18 * jax.random.normal(streams_of[4], (2, D), jnp.float32), 0.1, 1.9)
    gate_weight = gaussian(streams_of[5], (D, EXPERTS * H), D ** -0.5, 0.125, ((0, 16), (1, 16)))
    up_weight = gaussian(streams_of[6], (D, EXPERTS * H), D ** -0.5, 0.125, ((0, 16), (1, 16)))
    down_weight = gaussian(streams_of[7], (EXPERTS * H, D), H ** -0.5, 0.09375, ((0, 16), (1, 16)))
    return dict(tokens=tokens, modality=modality, local_expert=local_expert, combine_weight=combine_weight, norm_gain=norm_gain, gate_weight=gate_weight, up_weight=up_weight, down_weight=down_weight)


def reference(tokens, modality, local_expert, combine_weight, norm_gain, gate_weight, up_weight, down_weight):
    resid = tokens.astype(jnp.float32)
    root_mean = jnp.sqrt(lax.optimization_barrier(jnp.mean(resid * resid, axis=1, keepdims=True)) + 1e-05)
    row_gain = jnp.where(modality[:, None] == 0, norm_gain[0][None, :], norm_gain[1][None, :])
    normed = (resid / root_mean * row_gain).astype(jnp.bfloat16)
    route = modality * EXP_MOD + local_expert
    blocks = TOKENS // TOK_DEV
    routed = route.reshape(blocks, TOK_DEV)
    onehot = (routed[:, :, None] == jnp.arange(EXPERTS, dtype=jnp.int32)[None, None, :]).astype(jnp.int32)
    row_rank = lax.optimization_barrier(jnp.sum((jnp.cumsum(onehot, axis=1) - 1) * onehot, axis=2))
    block_ids = jnp.arange(blocks, dtype=jnp.int32)[:, None]
    slot_index = ((routed * blocks + block_ids) * CAP + row_rank).reshape(-1).astype(jnp.int32)
    token_ids = jnp.arange(TOKENS, dtype=jnp.int32)
    slot_table = jnp.full((EXPERTS * blocks * CAP,), TOKENS, dtype=jnp.int32).at[slot_index].set(token_ids)
    padded = jnp.concatenate([normed, jnp.zeros((1, D), jnp.bfloat16)], axis=0)
    gathered = padded[slot_table].reshape(EXPERTS, blocks * CAP, D)
    group = N_EXPERT // EXPERTS
    quarter = H // group

    def per_expert(expert_index):
        rows_e = lax.dynamic_index_in_dim(gathered, expert_index, 0, keepdims=False)
        total = jnp.zeros((blocks * CAP, D), jnp.float32)
        for part_index in range(group):
            first_col = (expert_index * H + part_index * quarter).astype(jnp.int32)
            gate_part = lax.dynamic_slice_in_dim(gate_weight, first_col, quarter, 1)
            up_part = lax.dynamic_slice_in_dim(up_weight, first_col, quarter, 1)
            down_part = lax.dynamic_slice_in_dim(down_weight, first_col, quarter, 0)
            gate_acts = jnp.dot(rows_e, gate_part, preferred_element_type=jnp.float32)
            up_acts = jnp.dot(rows_e, up_part, preferred_element_type=jnp.float32)
            hidden = (jax.nn.silu(gate_acts) * up_acts).astype(jnp.bfloat16)
            partial_out = jnp.dot(hidden, down_part, preferred_element_type=jnp.float32).astype(jnp.bfloat16)
            partial_out = lax.optimization_barrier(partial_out)
            total = total + partial_out.astype(jnp.float32)
        return total
    expert_sums = lax.map(per_expert, jnp.arange(EXPERTS, dtype=jnp.int32))
    moe_out = jnp.zeros((TOKENS + 1, D), jnp.float32).at[slot_table].add(expert_sums.reshape(-1, D))[:TOKENS]
    return (resid + combine_weight[:, None] * moe_out).astype(jnp.bfloat16)
```

```python
import jax
import jax.numpy as jnp
import numpy as np
from jax import lax
from jax.experimental import pallas as pl
from jax.experimental.pallas import tpu as pltpu
from jax.sharding import PartitionSpec as P

EXP_MOD = 2
EXPERTS = 4
CAP = 72
D = 2048
HID = 1024
ROWS = 16 * CAP
HALF = D // 2
BF = jnp.bfloat16
F32 = jnp.float32
REL = (0, -1, 1, 2)


def make_table():
    table = np.zeros((32, 17), np.int32)
    for core in range(2):
        for x in range(4):
            for y in range(4):
                for j, dv in enumerate(REL):
                    for i, du in enumerate(REL):
                        kx, ky = (x + du, y + dv) if core == 0 else (x + dv, y + du)
                        table[core * 16 + x * 4 + y, j * 4 + i] = kx % 4 * 4 + ky % 4
                table[core * 16 + x * 4 + y, 16] = core
    return table


TABLE = make_table()


def ring_perm(first, step):
    pairs = []
    for x in range(4):
        for y in range(4):
            for e in range(16):
                along_x = (e % 2 == 0) == first
                nx, ny = ((x + step) % 4, y) if along_x else (x, (y + step) % 4)
                pairs.append(((x * 4 + y) * 16 + e, (nx * 4 + ny) * 16 + e))
    return pairs


def shift(value, first, step):
    return lax.ppermute(value, ("dp", "expert"), ring_perm(first, step))


def core_swap(value):
    return lax.ppermute(value, "expert", [(e, e ^ 1) for e in range(16)])


def ring(value, first, rows):
    from_left = shift(value, first, 1)
    from_right = shift(value, first, -1)
    far_low = shift(from_left[: rows // 2], first, 1)
    far_high = shift(from_right[rows // 2 :], first, -1)
    return from_left, from_right, far_low, far_high


def pack_down(block):
    return block.reshape(16, 8, 8, 128).transpose(0, 2, 1, 3).reshape(128, 1024)


def unpack_down(block):
    return block.reshape(16, 8, 8, 128).transpose(0, 2, 1, 3).reshape(1024, 128)


def gather_weights(gate, up, down):
    own = jnp.concatenate([gate, up, pack_down(down)], axis=0)
    left, right, far_low, far_high = ring(own, True, 384)
    far = jnp.concatenate([far_low, far_high], axis=0)
    gu = jnp.concatenate([own[:256], left[:256], right[:256], far[:256]], axis=0)
    dn = jnp.concatenate(
        [down, unpack_down(left[256:]), unpack_down(right[256:]), unpack_down(far[256:])], axis=1
    )
    gu_pieces = (gu,) + ring(gu, False, 1024)
    dn_pieces = (dn,) + ring(dn, False, 1024)
    return gu_pieces, dn_pieces


M = 384


def ffn_body(tab, xa, xb, g0, g1, g2, g3, g4, d0, d1, d2, d3, d4, own_out, sib_out,
             xs, wg, wu, wd, hid, sem):
    core = tab[16]
    copies = []

    def go(src, dst, which):
        copy = pltpu.make_async_copy(src, dst, sem.at[which])
        copy.start()
        copies.append((which, copy))

    def wait(which):
        for w, copy in copies:
            if w == which:
                copy.wait()

    go(xa, xs.at[:, pl.ds(pl.multiple_of(core * HALF, HALF), HALF)], 0)
    go(xb, xs.at[:, pl.ds(pl.multiple_of((1 - core) * HALF, HALF), HALF)], 0)
    for j in range(4):
        for i in range(4):
            at = pl.multiple_of(tab[j * 4 + i] * 128, 128)
            if j < 3:
                src, base = (g0, g1, g2)[j], i * 256
            else:
                src, base = (g3, g4)[i // 2], (i % 2) * 256
            go(src.at[pl.ds(base, 128), :], wg.at[pl.ds(at, 128), :], 0)
            go(src.at[pl.ds(base + 128, 128), :], wu.at[pl.ds(at, 128), :], 0)
    for j in range(4):
        for i in range(4):
            at = pl.multiple_of(tab[j * 4 + i] * 128, 128)
            cols = pl.ds(i * 128, 128)
            if j < 3:
                go((d0, d1, d2)[j].at[:, cols], wd.at[:, pl.ds(at, 128)], 1)
            else:
                go(d3.at[:, cols], wd.at[pl.ds(0, 512), pl.ds(at, 128)], 1)
                go(d4.at[:, cols], wd.at[pl.ds(512, 512), pl.ds(at, 128)], 1)
    wait(0)

    def up_step(step, carry):
        m, n = step // 4, step % 4
        rows = pl.ds(pl.multiple_of(m * M, M), M)
        cols = pl.ds(pl.multiple_of(n * 256, 256), 256)
        xv = xs[rows, :]
        g = jnp.dot(xv, wg[:, cols], preferred_element_type=F32)
        u = jnp.dot(xv, wu[:, cols], preferred_element_type=F32)
        hid[rows, cols] = (g / (1.0 + jnp.exp(-g)) * u).astype(BF)
        return carry

    lax.fori_loop(0, (ROWS // M) * 4, up_step, 0)
    wait(1)

    def down_step(step, carry):
        m, n = step // 4, step % 4
        rows = pl.ds(pl.multiple_of(m * M, M), M)
        cols = pl.ds(pl.multiple_of(n * 256, 256), 256)
        hv = hid[rows, :]
        a = pl.multiple_of(core * HALF + n * 256, 256)
        b = pl.multiple_of((1 - core) * HALF + n * 256, 256)
        own_out[rows, cols] = jnp.dot(hv, wd[:, pl.ds(a, 256)], preferred_element_type=F32).astype(BF)
        sib_out[rows, cols] = jnp.dot(hv, wd[:, pl.ds(b, 256)], preferred_element_type=F32).astype(BF)
        return carry

    lax.fori_loop(0, (ROWS // M) * 4, down_step, 0)


def ffn(tab, xa, xb, gu_pieces, dn_pieces):
    hbm = pl.BlockSpec(memory_space=pl.ANY)
    out = jax.ShapeDtypeStruct((ROWS, HALF), BF)
    return pl.pallas_call(
        ffn_body,
        out_shape=(out, out),
        in_specs=[pl.BlockSpec(memory_space=pltpu.SMEM)] + [hbm] * 12,
        out_specs=(pl.BlockSpec(memory_space=pltpu.VMEM), pl.BlockSpec(memory_space=pltpu.VMEM)),
        scratch_shapes=[
            pltpu.VMEM((ROWS, D), BF),
            pltpu.VMEM((D, HID), BF),
            pltpu.VMEM((D, HID), BF),
            pltpu.VMEM((HID, D), BF),
            pltpu.VMEM((ROWS, HID), BF),
            pltpu.SemaphoreType.DMA((2,)),
        ],
        cost_estimate=pl.CostEstimate(
            flops=2 * ROWS * D * HID * 3, bytes_accessed=22_000_000, transcendentals=ROWS * HID
        ),
        name="ffn",
    )(tab, xa, xb, *gu_pieces, *dn_pieces)


def body(
    tokens, modality, local_expert, combine_weight, norm_gain, gate_weight, up_weight, down_weight
):
    dp = lax.axis_index("dp")
    core = lax.axis_index("expert") % 2
    tab = lax.dynamic_index_in_dim(jnp.asarray(TABLE), core * 16 + dp, 0, keepdims=False)

    gu_pieces, dn_pieces = gather_weights(gate_weight, up_weight, down_weight)

    resid = tokens.astype(F32)
    root_mean = jnp.sqrt(jnp.mean(resid * resid, axis=1, keepdims=True) + 1e-05)
    row_gain = jnp.where(modality[:, None] == 0, norm_gain[0][None, :], norm_gain[1][None, :])
    normed = (resid / root_mean * row_gain).astype(BF)
    route = modality * EXP_MOD + local_expert
    onehot = (route[:, None] == jnp.arange(EXPERTS, dtype=jnp.int32)[None, :]).astype(jnp.int32)
    row_rank = jnp.sum((jnp.cumsum(onehot, axis=0) - 1) * onehot, axis=1)
    position = route * CAP + row_rank
    placing = position[:, None] == jnp.arange(EXPERTS * CAP, dtype=jnp.int32)[None, :]
    buffer = jnp.einsum(
        "ts,td->sd", placing.astype(BF), normed, preferred_element_type=F32
    ).astype(BF)
    halves = buffer.reshape(EXPERTS, CAP, 2, HALF).transpose(0, 2, 1, 3)
    outgoing = jnp.broadcast_to(
        halves[:, None], (EXPERTS, 2, 2, CAP, HALF)
    ).reshape(16, CAP, HALF)
    arrival = lax.all_to_all(outgoing, "expert", split_axis=0, concat_axis=0, tiled=True).reshape(
        ROWS, HALF
    )
    sibling = core_swap(arrival)
    own_out, sib_out = ffn(tab, arrival, sibling, gu_pieces, dn_pieces)
    other = core_swap(sib_out)
    total = (own_out.astype(F32) + other.astype(F32)).astype(BF)
    returned = lax.all_to_all(
        total.reshape(16, CAP, HALF), "expert", split_axis=0, concat_axis=0, tiled=True
    )
    parts = returned.reshape(EXPERTS, 2, 2, CAP, HALF).astype(F32)
    summed = (parts[:, 0] + parts[:, 1]).transpose(0, 2, 1, 3).reshape(EXPERTS * CAP, D)
    moe_out = jnp.dot(placing.astype(F32), summed, precision=lax.Precision.HIGHEST)
    return (resid + combine_weight[:, None] * moe_out).astype(BF)


def solution(mesh):
    in_specs = (
        P(("dp", "expert"), None),
        P(("dp", "expert")),
        P(("dp", "expert")),
        P(("dp", "expert")),
        P(),
        P("dp", "expert"),
        P("dp", "expert"),
        P("expert", "dp"),
    )
    out_specs = P(("dp", "expert"), None)
    return jax.shard_map(body, mesh=mesh, in_specs=in_specs, out_specs=out_specs, check_vma=False)
```
